32 devices in a mesh: tx: 8 (over z, x), ty: 4 (over y, core).
Axes of the slice: x: 2, y: 2, z: 4, core: 2. Of those that a mesh axis runs over, the one named last changes fastest.
Arguments:
- dynamics_residual: float32 [6, 48, 48, 16], P(None, 'tx', 'ty'), may hold values from -6 to 6
- density: float32 [6, 48, 48, 16], P(None, 'tx', 'ty'), may hold values from 0.5 to 8
- diagonal_gain: float32 [6, 48, 48, 16], P(None, 'tx', 'ty'), may hold values from 0.05 to 2
- vertical_coupling: float32 [6, 48, 48, 16], P(None, 'tx', 'ty'), may hold values from 0.2 to 8
- edge_panel: int32 [6, 4], replicated, may hold values from 0 to 5, as said below
- edge_side: int32 [6, 4], replicated, may hold values from 0 to 3, as said below
- edge_flip: int32 [6, 4], replicated, may hold values from 0 to 1, as said below
Outputs:
- solution: float32 [6, 48, 48, 16], P(None, 'tx', 'ty')
- coarse_correction: float32 [6, 24, 24, 16], P(None, 'tx', 'ty')
The draws below stay inside these ranges and needn't reach their ends.
Inputs may be any that keep to these rules, and one draw needn't show every extreme that they name: The six panels are the faces of a cube, each with its own orientation and label: side s of panel p borders side edge_side[p, s] of panel edge_panel[p, s], the pairing is mutual, and no side borders a side of its own panel. `edge_side`: see edge_panel. `edge_flip`: equal on both sides of a bordering pair.
All inputs are finite; a program needn't handle non-finite values.
Results may differ from the reference program's by a relative error of at most 0.00005.
Values sent between devices are 32-bit elements; how exact they have to be, the bound alone decides.
A program may use at most 64 MiB of HBM per device.

```python
import math
import jax
import jax.numpy as jnp
import numpy as np

LEV = 16
NSIDE = 48


def frame_tables():
    anchors = np.array([[0, 0, 0], [0, 0, 1], [0, 0, 0], [0, 1, 0], [0, 0, 0], [1, 0, 0]])
    first_dirs = np.array([[1, 0, 0], [0, 1, 0], [0, 0, 1], [1, 0, 0], [0, 1, 0], [0, 0, 1]])
    second_dirs = np.array([[0, 1, 0], [1, 0, 0], [1, 0, 0], [0, 0, 1], [0, 0, 1], [0, 1, 0]])
    all_anchors = []
    all_first = []
    all_second = []
    for turn in range(4):
        all_anchors.append(anchors.copy())
        all_first.append(first_dirs.copy())
        all_second.append(second_dirs.copy())
        anchors, first_dirs, second_dirs = (anchors + first_dirs, second_dirs, -first_dirs)
    return (np.stack(all_anchors), np.stack(all_first), np.stack(all_second))


def edge_pairing(key):
    table_anchor, table_first, table_second = frame_tables()
    turns = jax.random.randint(jax.random.fold_in(key, 7), (6,), 0, 4).astype(jnp.int32)
    faces = jnp.arange(6)
    anchor = jnp.asarray(table_anchor, jnp.int32)[turns, faces]
    first_dir = jnp.asarray(table_first, jnp.int32)[turns, faces]
    second_dir = jnp.asarray(table_second, jnp.int32)[turns, faces]
    starts = jnp.stack([anchor, anchor + first_dir, anchor, anchor + second_dir], axis=1)
    ends = jnp.stack([anchor + second_dir, anchor + first_dir + second_dir, anchor + first_dir, anchor + first_dir + second_dir], axis=1)
    labels = jax.random.permutation(jax.random.fold_in(key, 11), 6).astype(jnp.int32)
    starts = jnp.zeros_like(starts).at[labels].set(starts).reshape(24, 3)
    ends = jnp.zeros_like(ends).at[labels].set(ends).reshape(24, 3)
    same = jnp.all(starts[:, None] == starts[None, :], axis=-1) & jnp.all(ends[:, None] == ends[None, :], axis=-1)
    opposite = jnp.all(starts[:, None] == ends[None, :], axis=-1) & jnp.all(ends[:, None] == starts[None, :], axis=-1)
    others = jnp.arange(24)[:, None] != jnp.arange(24)[None, :]
    matched = ((same | opposite) & others).astype(jnp.int32)
    partner = jnp.argmax(matched, axis=1).astype(jnp.int32)
    flip_codes = jnp.sum(opposite.astype(jnp.int32) * matched, axis=1).astype(jnp.int32)
    return (partner.reshape(6, 4), flip_codes.reshape(6, 4))


def draw_edge_panel(key, part):
    partner, flip_codes = edge_pairing(key)
    return (partner // 4).astype(jnp.int32)


def draw_edge_side(key, part):
    partner, flip_codes = edge_pairing(key)
    return (partner % 4).astype(jnp.int32)


def draw_edge_flip(key, part):
    partner, flip_codes = edge_pairing(key)
    return flip_codes.astype(jnp.int32)


def block_scale(stream_key, dims, shards, smallest, high):
    gain = 1.0
    for dim, shards_of in shards:
        heights = jax.random.uniform(jax.random.fold_in(jax.random.fold_in(stream_key, 6), dim), (shards_of,), jnp.float32, smallest / len(shards), high / len(shards))
        gain = gain * jnp.repeat(jnp.exp(heights), dims[dim] // shards_of).reshape((-1,) + (1,) * (len(dims) - 1 - dim))
    return gain


def centred(stream_key, extent, spread, limit, cuts=(), kind=jnp.bfloat16):
    entries = spread * jax.random.normal(stream_key, extent, jnp.float32)
    if cuts:
        entries = entries * block_scale(stream_key, extent, cuts, -0.22, 0.18)
    return jnp.clip(entries, -limit, limit).astype(kind)


def setup_inputs(seed: int = 0) -> dict:
    key_of = jax.random.split(jax.random.key(seed), 8)
    dynamics_residual = centred(key_of[0], (6, NSIDE, NSIDE, LEV), 1.0, 6.0, ((1, 8), (2, 4)), jnp.float32)
    density = jnp.clip(jnp.exp(math.log(8.0) - 2.7725887 * jax.random.uniform(key_of[1], (6, NSIDE, NSIDE, LEV), jnp.float32) ** block_scale(key_of[1], (6, NSIDE, NSIDE, LEV), ((1, 8), (2, 4)), -0.2, 0.2)), 0.5, 8.0)
    diagonal_gain = jnp.clip(jnp.exp(math.log(2.0) - 3.6888794 * jax.random.uniform(key_of[2], (6, NSIDE, NSIDE, LEV), jnp.float32) ** block_scale(key_of[2], (6, NSIDE, NSIDE, LEV), ((1, 8), (2, 4)), -0.2, 0.2)), 0.05, 2.0)
    vertical_coupling = jnp.clip(jnp.exp(math.log(8.0) - 3.6888794 * jax.random.uniform(key_of[3], (6, NSIDE, NSIDE, LEV), jnp.float32) ** block_scale(key_of[3], (6, NSIDE, NSIDE, LEV), ((1, 8), (2, 4)), -0.2, 0.2)), 0.2, 8.0)
    edge_panel = draw_edge_panel(jax.random.fold_in(key_of[7], 71), 0)
    edge_side = draw_edge_side(jax.random.fold_in(key_of[7], 71), 0)
    edge_flip = draw_edge_flip(jax.random.fold_in(key_of[7], 71), 0)
    return dict(dynamics_residual=dynamics_residual, density=density, diagonal_gain=diagonal_gain, vertical_coupling=vertical_coupling, edge_panel=edge_panel, edge_side=edge_side, edge_flip=edge_flip)


relaxation = 0.8


def lower_levels(values):
    return jnp.concatenate([jnp.zeros_like(values[..., :1]), values[..., :-1]], axis=-1)


def upper_levels(values):
    return jnp.concatenate([values[..., 1:], jnp.zeros_like(values[..., :1])], axis=-1)


def vertical_part(grid_field, vertical):
    return vertical * (grid_field - upper_levels(grid_field)) + lower_levels(vertical) * (grid_field - lower_levels(grid_field))


def diagonal_of(cell_gain, vertical, horizontal):
    return cell_gain + 4.0 * horizontal + vertical + lower_levels(vertical)


def neighbour_sum(padded):
    return padded[:, :-2, 1:-1] + padded[:, 2:, 1:-1] + padded[:, 1:-1, :-2] + padded[:, 1:-1, 2:]


def apply_operator(grid_field, padded, cell_gain, vertical, horizontal):
    return cell_gain * grid_field + horizontal * (4.0 * grid_field - neighbour_sum(padded)) + vertical_part(grid_field, vertical)


def restrict(values):
    shaped = values.reshape(values.shape[0], values.shape[1] // 2, 2, values.shape[2] // 2, 2, values.shape[3])
    return shaped.mean(axis=(2, 4))


def prolong(values):
    return jnp.repeat(jnp.repeat(values, 2, axis=1), 2, axis=2)


def panel_padded(grid_field, edge_panel, edge_side, edge_flip):
    strips = jnp.stack([grid_field[:, 0], grid_field[:, -1], grid_field[:, :, 0], grid_field[:, :, -1]])
    sources = strips[edge_side, edge_panel]
    rim_cells = jnp.where(edge_flip[:, :, None, None] == 1, sources[:, :, ::-1], sources)
    padded = jnp.pad(grid_field, ((0, 0), (1, 1), (1, 1), (0, 0)))
    padded = padded.at[:, 0, 1:-1].set(rim_cells[:, 0])
    padded = padded.at[:, -1, 1:-1].set(rim_cells[:, 1])
    padded = padded.at[:, 1:-1, 0].set(rim_cells[:, 2])
    padded = padded.at[:, 1:-1, -1].set(rim_cells[:, 3])
    return padded


def reference(dynamics_residual, density, diagonal_gain, vertical_coupling, edge_panel, edge_side, edge_flip):
    right_side = density * dynamics_residual
    fine_diagonal = diagonal_of(diagonal_gain, vertical_coupling, 1.0)
    smoothed = relaxation * right_side / fine_diagonal
    applied = apply_operator(smoothed, panel_padded(smoothed, edge_panel, edge_side, edge_flip), diagonal_gain, vertical_coupling, 1.0)
    coarse_rhs = restrict(right_side - applied)
    coarse_gain = restrict(diagonal_gain)
    coarse_vertical = restrict(vertical_coupling)
    coarse_diagonal = diagonal_of(coarse_gain, coarse_vertical, 0.25)
    coarse_guess = relaxation * coarse_rhs / coarse_diagonal
    coarse_applied = apply_operator(coarse_guess, panel_padded(coarse_guess, edge_panel, edge_side, edge_flip), coarse_gain, coarse_vertical, 0.25)
    coarse_correction = coarse_guess + relaxation * (coarse_rhs - coarse_applied) / coarse_diagonal
    corrected = smoothed + prolong(coarse_correction)
    final_applied = apply_operator(corrected, panel_padded(corrected, edge_panel, edge_side, edge_flip), diagonal_gain, vertical_coupling, 1.0)
    solution = corrected + relaxation * (right_side - final_applied) / fine_diagonal
    return solution, coarse_correction
```

```python
import functools

import jax
import jax.numpy as jnp
from jax import lax
from jax.experimental import pallas as pl
from jax.experimental.pallas import tpu as pltpu
from jax.sharding import PartitionSpec as P

MESH = pl.DeviceIdType.MESH
relaxation = 0.8
LANES = 128


def round_up(value, unit):
    return (value + unit - 1) // unit * unit


def kernel(
    nr,
    nc,
    res_hbm,
    den_hbm,
    gain_hbm,
    vert_hbm,
    panel_ref,
    side_ref,
    flip_ref,
    sol_ref,
    corr_ref,
    inp,
    packed,
    spread,
    st_row,
    st_col,
    nb_row,
    nb_col,
    rx_row,
    rx_col,
    in_sem,
    send_sem,
    nb_sem,
    row_sem,
    col_sem,
):
    panels, rows, cols, levels = sol_ref.shape
    half_r, half_c = rows // 2, cols // 2
    k = cols // rows
    height = spread.shape[1] // 2
    r = lax.axis_index("tx")
    c = lax.axis_index("ty")
    is_row = (r == 0) | (r == nr - 1)
    is_col = (c == 0) | (c == nc - 1)
    tr = r // (nr - 1)
    tc = c // (nc - 1)

    def messages(n):
        found = []
        found.append((r > 0, (r - 1, c), st_row.at[n, 0], nb_row.at[n, 1], nb_sem.at[n, 1]))
        found.append((r < nr - 1, (r + 1, c), st_row.at[n, 1], nb_row.at[n, 0], nb_sem.at[n, 0]))
        found.append((c > 0, (r, c - 1), st_col.at[n, 0], nb_col.at[n, 1], nb_sem.at[n, 3]))
        found.append((c < nc - 1, (r, c + 1), st_col.at[n, 1], nb_col.at[n, 0], nb_sem.at[n, 2]))
        for i in range(k):
            src = st_row.at[n, tr, i]
            for f in range(2):
                slot = 4 * f + tr
                i_dst = i if f == 0 else k - 1 - i
                c_dst = c if f == 0 else nc - 1 - c
                r_dst = k * c + i if f == 0 else nr - 1 - k * c - i
                for e in range(2):
                    found.append(
                        (
                            is_row,
                            (e * (nr - 1), c_dst),
                            src,
                            rx_row.at[n, slot, i_dst],
                            row_sem.at[n, slot, i_dst],
                        )
                    )
                    found.append(
                        (
                            is_row,
                            (r_dst, e * (nc - 1)),
                            src,
                            rx_col.at[n, slot],
                            col_sem.at[n, slot],
                        )
                    )
        src = st_col.at[n, tc]
        for f in range(2):
            slot = 4 * f + 2 + tc
            g = r if f == 0 else nr - 1 - r
            for e in range(2):
                found.append(
                    (
                        is_col,
                        (e * (nr - 1), g // k),
                        src,
                        rx_row.at[n, slot, g % k],
                        row_sem.at[n, slot, g % k],
                    )
                )
                found.append(
                    (is_col, (g, e * (nc - 1)), src, rx_col.at[n, slot], col_sem.at[n, slot])
                )
        return found

    def same(dest):
        return (dest[0] == r) & (dest[1] == c)

    barrier = pltpu.get_barrier_semaphore()
    expected = jnp.int32(0)
    for active, dest, _, _, _ in messages(0):
        go = active & jnp.logical_not(same(dest))
        expected = expected + go.astype(jnp.int32)

        @pl.when(go)
        def _():
            pl.semaphore_signal(barrier, inc=1, device_id=dest, device_id_type=MESH)

    loads = [
        pltpu.make_async_copy(source, inp.at[i], in_sem.at[i])
        for i, source in enumerate((den_hbm, res_hbm, gain_hbm, vert_hbm))
    ]
    for load in loads:
        load.start()

    lane = lax.broadcasted_iota(jnp.int32, (height, LANES), 1)
    sub = lax.broadcasted_iota(jnp.int32, (height, LANES), 0)
    level = lane % levels
    first_level = level == 0
    last_level = level == levels - 1

    def lower(x):
        return jnp.where(first_level, 0.0, pltpu.roll(x, 1, 1))

    def upper(x):
        return jnp.where(last_level, 0.0, pltpu.roll(x, LANES - 1, 1))

    seg_h = st_col.shape[2]
    seg_lane = lax.broadcasted_iota(jnp.int32, (seg_h, LANES), 1)

    def pick_tables(side):
        index = seg_lane
        code = jnp.zeros_like(seg_lane)
        for p in range(panels):
            here = seg_lane // levels == p
            index = jnp.where(here, panel_ref[p, side] * levels + seg_lane % levels, index)
            code = jnp.where(here, flip_ref[p, side] * 4 + side_ref[p, side], code)
        return index, code

    row_pick = pick_tables(tr)
    col_pick = pick_tables(2 + tc)

    for load in loads:
        load.wait()

    def pack(value):
        filler = jnp.zeros((rows, cols, LANES - panels * levels), jnp.float32)
        return jnp.concatenate([value[p] for p in range(panels)] + [filler], axis=-1)

    def split(which, value):
        packed[which, :, :cols, :] = value
        if packed.shape[2] > cols:
            packed[which, :, cols:, :] = jnp.zeros(
                (rows, packed.shape[2] - cols, LANES), jnp.float32
            )
        return [
            [packed[which, y, pl.ds(b, height, stride=2), :] for b in range(2)]
            for y in range(rows)
        ]

    every = [(y, b) for y in range(rows) for b in range(2)]

    def fine(fun):
        return [[fun(y, b) for b in range(2)] for y in range(rows)]

    right_side = split(0, pack(inp[0] * inp[1]))
    gain = split(1, pack(inp[2]))
    vertical = split(2, pack(inp[3]))
    low_vert = fine(lambda y, b: lower(vertical[y][b]))
    inverse = fine(
        lambda y, b: relaxation / (gain[y][b] + 4.0 + vertical[y][b] + low_vert[y][b])
    )
    smoothed = fine(lambda y, b: inverse[y][b] * right_side[y][b])

    def start(n):
        for m, (active, dest, src, dst, sem) in enumerate(messages(n)):
            mine = same(dest)

            @pl.when(active & jnp.logical_not(mine))
            def _():
                pltpu.make_async_remote_copy(
                    src_ref=src,
                    dst_ref=dst,
                    send_sem=send_sem.at[n, m],
                    recv_sem=sem,
                    device_id=dest,
                    device_id_type=MESH,
                ).start()

            if m >= 4:

                @pl.when(active & mine)
                def _():
                    pltpu.make_async_copy(src, dst, sem).start()

    def finish_sends(n):
        for m, (active, dest, src, dst, sem) in enumerate(messages(n)):

            @pl.when(active & jnp.logical_not(same(dest)))
            def _():
                pltpu.make_async_copy(src, src, send_sem.at[n, m]).wait()

    def mirrored(x, length):
        lines = [x[length - 1 - s : length - s] for s in range(length)]
        if seg_h > length:
            lines.append(jnp.zeros((seg_h - length, LANES), jnp.float32))
        return jnp.concatenate(lines, axis=0)

    def select(read, pick, length):
        index, code = pick
        parts = []
        for f in range(2):
            taken = jnp.zeros((seg_h, LANES), jnp.float32)
            for t in range(4):
                moved = jnp.take_along_axis(
                    read(4 * f + t), index, axis=1, mode="promise_in_bounds"
                )
                taken = jnp.where(code == 4 * f + t, moved, taken)
            parts.append(taken)
        return jnp.where(code >= 4, mirrored(parts[1], length), parts[0])

    def receive(n, length):
        def arrived(ref, sem):
            pltpu.make_async_copy(ref, ref, sem).wait()

        @pl.when(r > 0)
        def _():
            arrived(nb_row.at[n, 0], nb_sem.at[n, 0])

        @pl.when(r < nr - 1)
        def _():
            arrived(nb_row.at[n, 1], nb_sem.at[n, 1])

        @pl.when(c > 0)
        def _():
            arrived(nb_col.at[n, 0], nb_sem.at[n, 2])

        @pl.when(c < nc - 1)
        def _():
            arrived(nb_col.at[n, 1], nb_sem.at[n, 3])

        @pl.when(is_row)
        def _():
            for slot in range(8):
                for i in range(k):
                    arrived(rx_row.at[n, slot, i], row_sem.at[n, slot, i])
            for i in range(k):
                nb_row[n, tr, i] = select(lambda s: rx_row[n, s, i], row_pick, length)

        @pl.when(is_col)
        def _():
            for slot in range(8):
                arrived(rx_col.at[n, slot], col_sem.at[n, slot])
            nb_col[n, tc] = select(lambda s: rx_col[n, s], col_pick, length)

    def gathered(n, end, b):
        lines = [nb_row[n, end, i, b * half_r : (b + 1) * half_r, :] for i in range(k)]
        if height > half_c:
            lines.append(jnp.zeros((height - half_c, LANES), jnp.float32))
        return jnp.concatenate(lines, axis=0)

    def from_left(x, line):
        return jnp.where(sub == 0, line, pltpu.roll(x, 1, 0))

    def from_right(x, line):
        return jnp.where(sub == half_c - 1, line, pltpu.roll(x, height - 1, 0))

    for end, y in ((0, 0), (1, rows - 1)):
        for i in range(k):
            for b in range(2):
                st_row[0, end, i, b * half_r : (b + 1) * half_r, :] = smoothed[y][b][
                    i * half_r : (i + 1) * half_r
                ]
    for y in range(rows):
        at = (y % 2) * half_r + y // 2
        st_col[0, 0, at : at + 1, :] = smoothed[y][0][0:1]
        st_col[0, 1, at : at + 1, :] = smoothed[y][1][half_c - 1 : half_c]
    pl.semaphore_wait(barrier, expected)
    start(0)

    def inner(y, b):
        x = smoothed[y][b]
        total = vertical[y][b] * upper(x) + low_vert[y][b] * lower(x) + smoothed[y][1 - b]
        if y > 0:
            total = total + smoothed[y - 1][b]
        if y < rows - 1:
            total = total + smoothed[y + 1][b]
        return total

    partial = fine(inner)

    def block_mean(values, i):
        y = 2 * i
        return 0.25 * (values[y][0] + values[y][1] + values[y + 1][0] + values[y + 1][1])

    small = range(half_r)
    c_vert = [block_mean(vertical, i) for i in small]
    c_low = [lower(c_vert[i]) for i in small]
    c_inv = [relaxation / (block_mean(gain, i) + 1.0 + c_vert[i] + c_low[i]) for i in small]

    receive(0, rows)

    def outer(y, b):
        at = (y % 2) * half_r + y // 2
        if b == 0:
            total = partial[y][b] + from_left(smoothed[y][1], nb_col[0, 0, at : at + 1, :])
        else:
            total = partial[y][b] + from_right(smoothed[y][0], nb_col[0, 1, at : at + 1, :])
        if y == 0:
            total = total + gathered(0, 0, b)
        if y == rows - 1:
            total = total + gathered(0, 1, b)
        return total

    off = fine(outer)
    residual = fine(lambda y, b: (1.0 - relaxation) * right_side[y][b] + off[y][b])
    guess = [c_inv[i] * block_mean(residual, i) for i in small]

    def stage_coarse(n, values):
        for end, i in ((0, 0), (1, half_r - 1)):
            for piece in range(k):
                st_row[n, end, piece, :half_r, :] = values[i][
                    piece * half_r : (piece + 1) * half_r
                ]
        for i in small:
            st_col[n, 0, i : i + 1, :] = values[i][0:1]
            st_col[n, 1, i : i + 1, :] = values[i][half_c - 1 : half_c]

    stage_coarse(1, guess)
    start(1)
    c_partial = []
    for i in small:
        x = guess[i]
        beside = jnp.zeros_like(x)
        if i > 0:
            beside = beside + guess[i - 1]
        if i < half_r - 1:
            beside = beside + guess[i + 1]
        c_partial.append(
            (beside, c_vert[i] * upper(x) + c_low[i] * lower(x))
        )
    receive(1, half_r)
    correction = []
    for i in small:
        beside, column = c_partial[i]
        beside = beside + from_left(guess[i], nb_col[1, 0, i : i + 1, :])
        beside = beside + from_right(guess[i], nb_col[1, 1, i : i + 1, :])
        if i == 0:
            beside = beside + gathered(1, 0, 0)
        if i == half_r - 1:
            beside = beside + gathered(1, 1, 0)
        correction.append(
            (2.0 - relaxation) * guess[i] + c_inv[i] * (0.25 * beside + column)
        )

    stage_coarse(2, correction)
    start(2)
    c_up = [upper(x) for x in correction]
    c_down = [lower(x) for x in correction]

    def base(y, b):
        i = y // 2
        total = off[y][b] + 2.0 * correction[i]
        total = total + vertical[y][b] * c_up[i] + low_vert[y][b] * c_down[i]
        other = i - 1 if y % 2 == 0 else i + 1
        if 0 <= other < half_r:
            total = total + correction[other]
        return (
            (2.0 - relaxation) * smoothed[y][b] + (1.0 - relaxation) * correction[i],
            total,
        )

    bases = fine(base)
    for i in small:
        for p in range(panels):
            corr_ref[p, i] = correction[i][:half_c, p * levels : (p + 1) * levels]
    receive(2, half_r)
    left = [from_left(correction[i], nb_col[2, 0, i : i + 1, :]) for i in small]
    right = [from_right(correction[i], nb_col[2, 1, i : i + 1, :]) for i in small]
    top = gathered(2, 0, 0)
    bottom = gathered(2, 1, 0)
    for y, b in every:
        first, total = bases[y][b]
        total = total + (left if b == 0 else right)[y // 2]
        if y == 0:
            total = total + top
        if y == rows - 1:
            total = total + bottom
        spread[y, pl.ds(b, height, stride=2), :] = first + inverse[y][b] * total
    for p in range(panels):
        sol_ref[p] = spread[:, :cols, p * levels : (p + 1) * levels]
    for n in range(3):
        finish_sends(n)


def solution(mesh):
    nr, nc = mesh.shape["tx"], mesh.shape["ty"]

    def shards(residual, density, gain, vertical, edge_panel, edge_side, edge_flip):
        panels, rows, cols, levels = residual.shape
        k = cols // rows
        assert cols == k * rows and rows % 2 == 0 and panels * levels <= LANES
        seg_h = round_up(rows, 8)
        height = round_up(cols // 2, 8)
        tall = 2 * height
        f32 = jnp.float32
        return pl.pallas_call(
            functools.partial(kernel, nr, nc),
            out_shape=(
                jax.ShapeDtypeStruct(residual.shape, f32),
                jax.ShapeDtypeStruct((panels, rows // 2, cols // 2, levels), f32),
            ),
            in_specs=[pl.BlockSpec(memory_space=pl.ANY)] * 4
            + [pl.BlockSpec(memory_space=pltpu.SMEM)] * 3,
            out_specs=(pl.BlockSpec(memory_space=pltpu.VMEM),) * 2,
            scratch_shapes=[
                pltpu.VMEM((4, panels, rows, cols, levels), f32),
                pltpu.VMEM((3, rows, tall, LANES), f32),
                pltpu.VMEM((rows, tall, LANES), f32),
                pltpu.VMEM((3, 2, k, seg_h, LANES), f32),
                pltpu.VMEM((3, 2, seg_h, LANES), f32),
                pltpu.VMEM((3, 2, k, seg_h, LANES), f32),
                pltpu.VMEM((3, 2, seg_h, LANES), f32),
                pltpu.VMEM((3, 8, k, seg_h, LANES), f32),
                pltpu.VMEM((3, 8, seg_h, LANES), f32),
                pltpu.SemaphoreType.DMA((4,)),
                pltpu.SemaphoreType.DMA((3, 4 + 8 * k + 4 + 4)),
                pltpu.SemaphoreType.DMA((3, 4)),
                pltpu.SemaphoreType.DMA((3, 8, k)),
                pltpu.SemaphoreType.DMA((3, 8)),
            ],
            compiler_params=pltpu.CompilerParams(collective_id=0, has_side_effects=True),
        )(residual, density, gain, vertical, edge_panel, edge_side, edge_flip)

    fields = P(None, "tx", "ty", None)
    return jax.shard_map(
        shards,
        mesh=mesh,
        in_specs=(fields,) * 4 + (P(),) * 3,
        out_specs=(fields, fields),
        check_vma=False,
    )
```

```python
import functools

import jax
import jax.numpy as jnp
from jax import lax
from jax.experimental import pallas as pl
from jax.experimental.pallas import tpu as pltpu
from jax.sharding import PartitionSpec as P

MESH = pl.DeviceIdType.MESH
relaxation = 0.8
LANES = 128


def round_up(value, unit):
    return (value + unit - 1) // unit * unit


def kernel(
    nr,
    nc,
    res_hbm,
    den_hbm,
    gain_hbm,
    vert_hbm,
    panel_ref,
    side_ref,
    flip_ref,
    sol_ref,
    corr_ref,
    inp,
    packed,
    spread,
    st_row,
    st_col,
    nb_row,
    nb_col,
    rx_row,
    rx_col,
    in_sem,
    send_sem,
    nb_sem,
    row_sem,
    col_sem,
):
    panels, rows, cols, levels = sol_ref.shape
    half_r, half_c = rows // 2, cols // 2
    k = cols // rows
    height = spread.shape[1] // 2
    r = lax.axis_index("tx")
    c = lax.axis_index("ty")
    is_row = (r == 0) | (r == nr - 1)
    is_col = (c == 0) | (c == nc - 1)
    tr = r // (nr - 1)
    tc = c // (nc - 1)

    def messages(n):
        found = []
        found.append((r > 0, (r - 1, c), st_row.at[n, 0], nb_row.at[n, 1], nb_sem.at[n, 1]))
        found.append((r < nr - 1, (r + 1, c), st_row.at[n, 1], nb_row.at[n, 0], nb_sem.at[n, 0]))
        found.append((c > 0, (r, c - 1), st_col.at[n, 0], nb_col.at[n, 1], nb_sem.at[n, 3]))
        found.append((c < nc - 1, (r, c + 1), st_col.at[n, 1], nb_col.at[n, 0], nb_sem.at[n, 2]))
        for i in range(k):
            src = st_row.at[n, tr, i]
            for f in range(2):
                slot = 4 * f + tr
                i_dst = i if f == 0 else k - 1 - i
                c_dst = c if f == 0 else nc - 1 - c
                r_dst = k * c + i if f == 0 else nr - 1 - k * c - i
                for e in range(2):
                    found.append(
                        (
                            is_row,
                            (e * (nr - 1), c_dst),
                            src,
                            rx_row.at[n, slot, i_dst],
                            row_sem.at[n, slot, i_dst],
                        )
                    )
                    found.append(
                        (
                            is_row,
                            (r_dst, e * (nc - 1)),
                            src,
                            rx_col.at[n, slot],
                            col_sem.at[n, slot],
                        )
                    )
        src = st_col.at[n, tc]
        for f in range(2):
            slot = 4 * f + 2 + tc
            g = r if f == 0 else nr - 1 - r
            for e in range(2):
                found.append(
                    (
                        is_col,
                        (e * (nr - 1), g // k),
                        src,
                        rx_row.at[n, slot, g % k],
                        row_sem.at[n, slot, g % k],
                    )
                )
                found.append(
                    (is_col, (g, e * (nc - 1)), src, rx_col.at[n, slot], col_sem.at[n, slot])
                )
        return found

    def same(dest):
        return (dest[0] == r) & (dest[1] == c)

    barrier = pltpu.get_barrier_semaphore()
    expected = jnp.int32(0)
    for active, dest, _, _, _ in messages(0):
        go = active & jnp.logical_not(same(dest))
        expected = expected + go.astype(jnp.int32)

        @pl.when(go)
        def _():
            pl.semaphore_signal(barrier, inc=1, device_id=dest, device_id_type=MESH)

    loads = [
        pltpu.make_async_copy(source, inp.at[i], in_sem.at[i])
        for i, source in enumerate((den_hbm, res_hbm, gain_hbm, vert_hbm))
    ]
    for load in loads:
        load.start()

    lane = lax.broadcasted_iota(jnp.int32, (height, LANES), 1)
    sub = lax.broadcasted_iota(jnp.int32, (height, LANES), 0)
    level = lane % levels
    first_level = level == 0
    last_level = level == levels - 1

    def lower(x):
        return jnp.where(first_level, 0.0, pltpu.roll(x, 1, 1))

    def upper(x):
        return jnp.where(last_level, 0.0, pltpu.roll(x, LANES - 1, 1))

    seg_h = st_col.shape[2]
    seg_lane = lax.broadcasted_iota(jnp.int32, (seg_h, LANES), 1)

    def pick_tables(side):
        index = seg_lane
        code = jnp.zeros_like(seg_lane)
        for p in range(panels):
            here = seg_lane // levels == p
            index = jnp.where(here, panel_ref[side, p] * levels + seg_lane % levels, index)
            code = jnp.where(here, flip_ref[side, p] * 4 + side_ref[side, p], code)
        return index, code

    row_pick = pick_tables(tr)
    col_pick = pick_tables(2 + tc)

    for load in loads:
        load.wait()

    def pack(value):
        filler = jnp.zeros((rows, cols, LANES - panels * levels), jnp.float32)
        return jnp.concatenate([value[p] for p in range(panels)] + [filler], axis=-1)

    def split(which, value):
        packed[which, :, :cols, :] = value
        if packed.shape[2] > cols:
            packed[which, :, cols:, :] = jnp.zeros(
                (rows, packed.shape[2] - cols, LANES), jnp.float32
            )
        return [
            [packed[which, y, pl.ds(b, height, stride=2), :] for b in range(2)]
            for y in range(rows)
        ]

    every = [(y, b) for y in range(rows) for b in range(2)]

    def fine(fun):
        return [[fun(y, b) for b in range(2)] for y in range(rows)]

    right_side = split(0, pack(inp[0] * inp[1]))
    gain = split(1, pack(inp[2]))
    vertical = split(2, pack(inp[3]))
    low_vert = fine(lambda y, b: lower(vertical[y][b]))
    inverse = fine(
        lambda y, b: relaxation / (gain[y][b] + 4.0 + vertical[y][b] + low_vert[y][b])
    )
    smoothed = fine(lambda y, b: inverse[y][b] * right_side[y][b])

    def start(n):
        for m, (active, dest, src, dst, sem) in enumerate(messages(n)):
            mine = same(dest)

            @pl.when(active & jnp.logical_not(mine))
            def _():
                pltpu.make_async_remote_copy(
                    src_ref=src,
                    dst_ref=dst,
                    send_sem=send_sem.at[n, m],
                    recv_sem=sem,
                    device_id=dest,
                    device_id_type=MESH,
                ).start()

            if m >= 4:

                @pl.when(active & mine)
                def _():
                    pltpu.make_async_copy(src, dst, sem).start()

    def finish_sends(n):
        for m, (active, dest, src, dst, sem) in enumerate(messages(n)):

            @pl.when(active & jnp.logical_not(same(dest)))
            def _():
                pltpu.make_async_copy(src, src, send_sem.at[n, m]).wait()

    def mirrored(x, length):
        lines = [x[length - 1 - s : length - s] for s in range(length)]
        if seg_h > length:
            lines.append(jnp.zeros((seg_h - length, LANES), jnp.float32))
        return jnp.concatenate(lines, axis=0)

    def select(read, pick, length):
        index, code = pick
        parts = []
        for f in range(2):
            taken = jnp.zeros((seg_h, LANES), jnp.float32)
            for t in range(4):
                moved = jnp.take_along_axis(
                    read(4 * f + t), index, axis=1, mode="promise_in_bounds"
                )
                taken = jnp.where(code == 4 * f + t, moved, taken)
            parts.append(taken)
        return jnp.where(code >= 4, mirrored(parts[1], length), parts[0])

    def receive(n, length):
        def arrived(ref, sem):
            pltpu.make_async_copy(ref, ref, sem).wait()

        @pl.when(r > 0)
        def _():
            arrived(nb_row.at[n, 0], nb_sem.at[n, 0])

        @pl.when(r < nr - 1)
        def _():
            arrived(nb_row.at[n, 1], nb_sem.at[n, 1])

        @pl.when(c > 0)
        def _():
            arrived(nb_col.at[n, 0], nb_sem.at[n, 2])

        @pl.when(c < nc - 1)
        def _():
            arrived(nb_col.at[n, 1], nb_sem.at[n, 3])

        @pl.when(is_row)
        def _():
            for slot in range(8):
                for i in range(k):
                    arrived(rx_row.at[n, slot, i], row_sem.at[n, slot, i])
            for i in range(k):
                nb_row[n, tr, i] = select(lambda s: rx_row[n, s, i], row_pick, length)

        @pl.when(is_col)
        def _():
            for slot in range(8):
                arrived(rx_col.at[n, slot], col_sem.at[n, slot])
            nb_col[n, tc] = select(lambda s: rx_col[n, s], col_pick, length)

    def gathered(n, end, b):
        lines = [nb_row[n, end, i, b * half_r : (b + 1) * half_r, :] for i in range(k)]
        if height > half_c:
            lines.append(jnp.zeros((height - half_c, LANES), jnp.float32))
        return jnp.concatenate(lines, axis=0)

    def from_left(x, line):
        return jnp.where(sub == 0, line, pltpu.roll(x, 1, 0))

    def from_right(x, line):
        return jnp.where(sub == half_c - 1, line, pltpu.roll(x, height - 1, 0))

    for end, y in ((0, 0), (1, rows - 1)):
        for i in range(k):
            for b in range(2):
                st_row[0, end, i, b * half_r : (b + 1) * half_r, :] = smoothed[y][b][
                    i * half_r : (i + 1) * half_r
                ]
    for y in range(rows):
        at = (y % 2) * half_r + y // 2
        st_col[0, 0, at : at + 1, :] = smoothed[y][0][0:1]
        st_col[0, 1, at : at + 1, :] = smoothed[y][1][half_c - 1 : half_c]
    pl.semaphore_wait(barrier, expected)
    start(0)

    def inner(y, b):
        x = smoothed[y][b]
        total = vertical[y][b] * upper(x) + low_vert[y][b] * lower(x) + smoothed[y][1 - b]
        if y > 0:
            total = total + smoothed[y - 1][b]
        if y < rows - 1:
            total = total + smoothed[y + 1][b]
        return total

    partial = fine(inner)

    def block_mean(values, i):
        y = 2 * i
        return 0.25 * (values[y][0] + values[y][1] + values[y + 1][0] + values[y + 1][1])

    small = range(half_r)
    c_vert = [block_mean(vertical, i) for i in small]
    c_low = [lower(c_vert[i]) for i in small]
    c_inv = [relaxation / (block_mean(gain, i) + 1.0 + c_vert[i] + c_low[i]) for i in small]

    receive(0, rows)

    def outer(y, b):
        at = (y % 2) * half_r + y // 2
        if b == 0:
            total = partial[y][b] + from_left(smoothed[y][1], nb_col[0, 0, at : at + 1, :])
        else:
            total = partial[y][b] + from_right(smoothed[y][0], nb_col[0, 1, at : at + 1, :])
        if y == 0:
            total = total + gathered(0, 0, b)
        if y == rows - 1:
            total = total + gathered(0, 1, b)
        return total

    off = fine(outer)
    residual = fine(lambda y, b: (1.0 - relaxation) * right_side[y][b] + off[y][b])
    guess = [c_inv[i] * block_mean(residual, i) for i in small]

    def stage_coarse(n, values):
        for end, i in ((0, 0), (1, half_r - 1)):
            for piece in range(k):
                st_row[n, end, piece, :half_r, :] = values[i][
                    piece * half_r : (piece + 1) * half_r
                ]
        for i in small:
            st_col[n, 0, i : i + 1, :] = values[i][0:1]
            st_col[n, 1, i : i + 1, :] = values[i][half_c - 1 : half_c]

    stage_coarse(1, guess)
    start(1)
    c_partial = []
    for i in small:
        x = guess[i]
        beside = jnp.zeros_like(x)
        if i > 0:
            beside = beside + guess[i - 1]
        if i < half_r - 1:
            beside = beside + guess[i + 1]
        c_partial.append(
            (beside, c_vert[i] * upper(x) + c_low[i] * lower(x))
        )
    receive(1, half_r)
    correction = []
    for i in small:
        beside, column = c_partial[i]
        beside = beside + from_left(guess[i], nb_col[1, 0, i : i + 1, :])
        beside = beside + from_right(guess[i], nb_col[1, 1, i : i + 1, :])
        if i == 0:
            beside = beside + gathered(1, 0, 0)
        if i == half_r - 1:
            beside = beside + gathered(1, 1, 0)
        correction.append(
            (2.0 - relaxation) * guess[i] + c_inv[i] * (0.25 * beside + column)
        )

    stage_coarse(2, correction)
    start(2)
    c_up = [upper(x) for x in correction]
    c_down = [lower(x) for x in correction]

    def base(y, b):
        i = y // 2
        total = off[y][b] + 2.0 * correction[i]
        total = total + vertical[y][b] * c_up[i] + low_vert[y][b] * c_down[i]
        other = i - 1 if y % 2 == 0 else i + 1
        if 0 <= other < half_r:
            total = total + correction[other]
        return (
            (2.0 - relaxation) * smoothed[y][b] + (1.0 - relaxation) * correction[i],
            total,
        )

    bases = fine(base)
    for i in small:
        for p in range(panels):
            corr_ref[p, i] = correction[i][:half_c, p * levels : (p + 1) * levels]
    receive(2, half_r)
    left = [from_left(correction[i], nb_col[2, 0, i : i + 1, :]) for i in small]
    right = [from_right(correction[i], nb_col[2, 1, i : i + 1, :]) for i in small]
    top = gathered(2, 0, 0)
    bottom = gathered(2, 1, 0)
    for y, b in every:
        first, total = bases[y][b]
        total = total + (left if b == 0 else right)[y // 2]
        if y == 0:
            total = total + top
        if y == rows - 1:
            total = total + bottom
        spread[y, pl.ds(b, height, stride=2), :] = first + inverse[y][b] * total
    for p in range(panels):
        sol_ref[p] = spread[:, :cols, p * levels : (p + 1) * levels]
    for n in range(3):
        finish_sends(n)


def solution(mesh):
    nr, nc = mesh.shape["tx"], mesh.shape["ty"]

    def shards(residual, density, gain, vertical, edge_panel, edge_side, edge_flip):
        panels, rows, cols, levels = residual.shape
        k = cols // rows
        assert cols == k * rows and rows % 2 == 0 and panels * levels <= LANES
        seg_h = round_up(rows, 8)
        height = round_up(cols // 2, 8)
        tall = 2 * height
        f32 = jnp.float32
        return pl.pallas_call(
            functools.partial(kernel, nr, nc),
            out_shape=(
                jax.ShapeDtypeStruct(residual.shape, f32),
                jax.ShapeDtypeStruct((panels, rows // 2, cols // 2, levels), f32),
            ),
            in_specs=[pl.BlockSpec(memory_space=pl.ANY)] * 4
            + [pl.BlockSpec(memory_space=pltpu.SMEM)] * 3,
            out_specs=(pl.BlockSpec(memory_space=pltpu.VMEM),) * 2,
            scratch_shapes=[
                pltpu.VMEM((4, panels, rows, cols, levels), f32),
                pltpu.VMEM((3, rows, tall, LANES), f32),
                pltpu.VMEM((rows, tall, LANES), f32),
                pltpu.VMEM((3, 2, k, seg_h, LANES), f32),
                pltpu.VMEM((3, 2, seg_h, LANES), f32),
                pltpu.VMEM((3, 2, k, seg_h, LANES), f32),
                pltpu.VMEM((3, 2, seg_h, LANES), f32),
                pltpu.VMEM((3, 8, k, seg_h, LANES), f32),
                pltpu.VMEM((3, 8, seg_h, LANES), f32),
                pltpu.SemaphoreType.DMA((4,)),
                pltpu.SemaphoreType.DMA((3, 4 + 8 * k + 4 + 4)),
                pltpu.SemaphoreType.DMA((3, 4)),
                pltpu.SemaphoreType.DMA((3, 8, k)),
                pltpu.SemaphoreType.DMA((3, 8)),
            ],
            compiler_params=pltpu.CompilerParams(collective_id=0, has_side_effects=True),
        )(residual, density, gain, vertical, edge_panel.T, edge_side.T, edge_flip.T)

    fields = P(None, "tx", "ty", None)
    return jax.shard_map(
        shards,
        mesh=mesh,
        in_specs=(fields,) * 4 + (P(),) * 3,
        out_specs=(fields, fields),
        check_vma=False,
    )
```

```python
import functools

import jax
import jax.numpy as jnp
from jax import lax
from jax.experimental import pallas as pl
from jax.experimental.pallas import tpu as pltpu
from jax.sharding import PartitionSpec as P

MESH = pl.DeviceIdType.MESH
relaxation = 0.8
LANES = 128


def round_up(value, unit):
    return (value + unit - 1) // unit * unit


def kernel(
    nr,
    nc,
    res_hbm,
    den_hbm,
    gain_hbm,
    vert_hbm,
    panel_ref,
    side_ref,
    flip_ref,
    sol_ref,
    corr_ref,
    inp,
    packed,
    spread,
    st_row,
    st_col,
    nb_row,
    nb_col,
    rx_row,
    rx_col,
    in_sem,
    send_sem,
    nb_sem,
    row_sem,
    col_sem,
):
    panels, rows, cols, levels = sol_ref.shape
    half_r, half_c = rows // 2, cols // 2
    k = cols // rows
    height = spread.shape[1] // 2
    r = lax.axis_index("tx")
    c = lax.axis_index("ty")
    is_row = (r == 0) | (r == nr - 1)
    is_col = (c == 0) | (c == nc - 1)
    tr = r // (nr - 1)
    tc = c // (nc - 1)

    def messages(n):
        found = []
        for i in range(k):
            src = st_row.at[n, tr, i]
            for f in range(2):
                slot = 4 * f + tr
                i_dst = i if f == 0 else k - 1 - i
                c_dst = c if f == 0 else nc - 1 - c
                r_dst = k * c + i if f == 0 else nr - 1 - k * c - i
                for e in range(2):
                    found.append(
                        (
                            is_row,
                            (e * (nr - 1), c_dst),
                            src,
                            rx_row.at[n, slot, i_dst],
                            row_sem.at[n, slot, i_dst],
                        )
                    )
                    found.append(
                        (
                            is_row,
                            (r_dst, e * (nc - 1)),
                            src,
                            rx_col.at[n, slot],
                            col_sem.at[n, slot],
                        )
                    )
        src = st_col.at[n, tc]
        for f in range(2):
            slot = 4 * f + 2 + tc
            g = r if f == 0 else nr - 1 - r
            for e in range(2):
                found.append(
                    (
                        is_col,
                        (e * (nr - 1), g // k),
                        src,
                        rx_row.at[n, slot, g % k],
                        row_sem.at[n, slot, g % k],
                    )
                )
                found.append(
                    (is_col, (g, e * (nc - 1)), src, rx_col.at[n, slot], col_sem.at[n, slot])
                )
        found.append((r > 0, (r - 1, c), st_row.at[n, 0], nb_row.at[n, 1], nb_sem.at[n, 1]))
        found.append((r < nr - 1, (r + 1, c), st_row.at[n, 1], nb_row.at[n, 0], nb_sem.at[n, 0]))
        found.append((c > 0, (r, c - 1), st_col.at[n, 0], nb_col.at[n, 1], nb_sem.at[n, 3]))
        found.append((c < nc - 1, (r, c + 1), st_col.at[n, 1], nb_col.at[n, 0], nb_sem.at[n, 2]))
        return found

    def same(dest):
        return (dest[0] == r) & (dest[1] == c)

    barrier = pltpu.get_barrier_semaphore()
    expected = jnp.int32(0)
    for active, dest, _, _, _ in messages(0):
        go = active & jnp.logical_not(same(dest))
        expected = expected + go.astype(jnp.int32)

        @pl.when(go)
        def _():
            pl.semaphore_signal(barrier, inc=1, device_id=dest, device_id_type=MESH)

    loads = [
        pltpu.make_async_copy(source, inp.at[i], in_sem.at[i])
        for i, source in enumerate((den_hbm, res_hbm, gain_hbm, vert_hbm))
    ]
    for load in loads:
        load.start()

    lane = lax.broadcasted_iota(jnp.int32, (height, LANES), 1)
    sub = lax.broadcasted_iota(jnp.int32, (height, LANES), 0)
    level = lane % levels
    first_level = level == 0
    last_level = level == levels - 1

    def lower(x):
        return jnp.where(first_level, 0.0, pltpu.roll(x, 1, 1))

    def upper(x):
        return jnp.where(last_level, 0.0, pltpu.roll(x, LANES - 1, 1))

    seg_h = st_col.shape[2]
    seg_lane = lax.broadcasted_iota(jnp.int32, (seg_h, LANES), 1)

    def pick_tables(side):
        index = seg_lane
        code = jnp.zeros_like(seg_lane)
        for p in range(panels):
            here = seg_lane // levels == p
            index = jnp.where(here, panel_ref[side, p] * levels + seg_lane % levels, index)
            code = jnp.where(here, flip_ref[side, p] * 4 + side_ref[side, p], code)
        return index, code

    row_pick = pick_tables(tr)
    col_pick = pick_tables(2 + tc)

    for load in loads:
        load.wait()

    def pack(value):
        filler = jnp.zeros((rows, cols, LANES - panels * levels), jnp.float32)
        return jnp.concatenate([value[p] for p in range(panels)] + [filler], axis=-1)

    def split(which, value):
        packed[which, :, :cols, :] = value
        if packed.shape[2] > cols:
            packed[which, :, cols:, :] = jnp.zeros(
                (rows, packed.shape[2] - cols, LANES), jnp.float32
            )
        return [
            [packed[which, y, pl.ds(b, height, stride=2), :] for b in range(2)]
            for y in range(rows)
        ]

    every = [(y, b) for y in range(rows) for b in range(2)]

    def fine(fun):
        return [[fun(y, b) for b in range(2)] for y in range(rows)]

    right_side = split(0, pack(inp[0] * inp[1]))
    gain = split(1, pack(inp[2]))
    vertical = split(2, pack(inp[3]))
    low_vert = fine(lambda y, b: lower(vertical[y][b]))
    inverse = fine(
        lambda y, b: relaxation / (gain[y][b] + 4.0 + vertical[y][b] + low_vert[y][b])
    )
    smoothed = fine(lambda y, b: inverse[y][b] * right_side[y][b])

    def start(n):
        for m, (active, dest, src, dst, sem) in enumerate(messages(n)):
            mine = same(dest)

            @pl.when(active & jnp.logical_not(mine))
            def _():
                pltpu.make_async_remote_copy(
                    src_ref=src,
                    dst_ref=dst,
                    send_sem=send_sem.at[n, m],
                    recv_sem=sem,
                    device_id=dest,
                    device_id_type=MESH,
                ).start()

            if m < 8 * k + 8:

                @pl.when(active & mine)
                def _():
                    pltpu.make_async_copy(src, dst, sem).start()

    def finish_sends(n):
        for m, (active, dest, src, dst, sem) in enumerate(messages(n)):

            @pl.when(active & jnp.logical_not(same(dest)))
            def _():
                pltpu.make_async_copy(src, src, send_sem.at[n, m]).wait()

    def mirrored(x, length):
        lines = [x[length - 1 - s : length - s] for s in range(length)]
        if seg_h > length:
            lines.append(jnp.zeros((seg_h - length, LANES), jnp.float32))
        return jnp.concatenate(lines, axis=0)

    def select(read, pick, length):
        index, code = pick
        parts = []
        for f in range(2):
            taken = jnp.zeros((seg_h, LANES), jnp.float32)
            for t in range(4):
                moved = jnp.take_along_axis(
                    read(4 * f + t), index, axis=1, mode="promise_in_bounds"
                )
                taken = jnp.where(code == 4 * f + t, moved, taken)
            parts.append(taken)
        return jnp.where(code >= 4, mirrored(parts[1], length), parts[0])

    def receive(n, length):
        def arrived(ref, sem):
            pltpu.make_async_copy(ref, ref, sem).wait()

        @pl.when(r > 0)
        def _():
            arrived(nb_row.at[n, 0], nb_sem.at[n, 0])

        @pl.when(r < nr - 1)
        def _():
            arrived(nb_row.at[n, 1], nb_sem.at[n, 1])

        @pl.when(c > 0)
        def _():
            arrived(nb_col.at[n, 0], nb_sem.at[n, 2])

        @pl.when(c < nc - 1)
        def _():
            arrived(nb_col.at[n, 1], nb_sem.at[n, 3])

        @pl.when(is_row)
        def _():
            for slot in range(8):
                for i in range(k):
                    arrived(rx_row.at[n, slot, i], row_sem.at[n, slot, i])
            for i in range(k):
                nb_row[n, tr, i] = select(lambda s: rx_row[n, s, i], row_pick, length)

        @pl.when(is_col)
        def _():
            for slot in range(8):
                arrived(rx_col.at[n, slot], col_sem.at[n, slot])
            nb_col[n, tc] = select(lambda s: rx_col[n, s], col_pick, length)

    def gathered(n, end, b):
        lines = [nb_row[n, end, i, b * half_r : (b + 1) * half_r, :] for i in range(k)]
        if height > half_c:
            lines.append(jnp.zeros((height - half_c, LANES), jnp.float32))
        return jnp.concatenate(lines, axis=0)

    def from_left(x, line):
        return jnp.where(sub == 0, line, pltpu.roll(x, 1, 0))

    def from_right(x, line):
        return jnp.where(sub == half_c - 1, line, pltpu.roll(x, height - 1, 0))

    for end, y in ((0, 0), (1, rows - 1)):
        for i in range(k):
            for b in range(2):
                st_row[0, end, i, b * half_r : (b + 1) * half_r, :] = smoothed[y][b][
                    i * half_r : (i + 1) * half_r
                ]
    for y in range(rows):
        at = (y % 2) * half_r + y // 2
        st_col[0, 0, at : at + 1, :] = smoothed[y][0][0:1]
        st_col[0, 1, at : at + 1, :] = smoothed[y][1][half_c - 1 : half_c]
    pl.semaphore_wait(barrier, expected)
    start(0)

    def inner(y, b):
        x = smoothed[y][b]
        total = vertical[y][b] * upper(x) + low_vert[y][b] * lower(x) + smoothed[y][1 - b]
        if y > 0:
            total = total + smoothed[y - 1][b]
        if y < rows - 1:
            total = total + smoothed[y + 1][b]
        return total

    partial = fine(inner)

    def block_mean(values, i):
        y = 2 * i
        return 0.25 * (values[y][0] + values[y][1] + values[y + 1][0] + values[y + 1][1])

    small = range(half_r)
    c_vert = [block_mean(vertical, i) for i in small]
    c_low = [lower(c_vert[i]) for i in small]
    c_inv = [relaxation / (block_mean(gain, i) + 1.0 + c_vert[i] + c_low[i]) for i in small]

    receive(0, rows)

    def outer(y, b):
        at = (y % 2) * half_r + y // 2
        if b == 0:
            total = partial[y][b] + from_left(smoothed[y][1], nb_col[0, 0, at : at + 1, :])
        else:
            total = partial[y][b] + from_right(smoothed[y][0], nb_col[0, 1, at : at + 1, :])
        if y == 0:
            total = total + gathered(0, 0, b)
        if y == rows - 1:
            total = total + gathered(0, 1, b)
        return total

    off = fine(outer)
    residual = fine(lambda y, b: (1.0 - relaxation) * right_side[y][b] + off[y][b])
    guess = [c_inv[i] * block_mean(residual, i) for i in small]

    def stage_coarse(n, values):
        for end, i in ((0, 0), (1, half_r - 1)):
            for piece in range(k):
                st_row[n, end, piece, :half_r, :] = values[i][
                    piece * half_r : (piece + 1) * half_r
                ]
        for i in small:
            st_col[n, 0, i : i + 1, :] = values[i][0:1]
            st_col[n, 1, i : i + 1, :] = values[i][half_c - 1 : half_c]

    stage_coarse(1, guess)
    start(1)
    c_partial = []
    for i in small:
        x = guess[i]
        beside = jnp.zeros_like(x)
        if i > 0:
            beside = beside + guess[i - 1]
        if i < half_r - 1:
            beside = beside + guess[i + 1]
        c_partial.append(
            (beside, c_vert[i] * upper(x) + c_low[i] * lower(x))
        )
    receive(1, half_r)
    correction = []
    for i in small:
        beside, column = c_partial[i]
        beside = beside + from_left(guess[i], nb_col[1, 0, i : i + 1, :])
        beside = beside + from_right(guess[i], nb_col[1, 1, i : i + 1, :])
        if i == 0:
            beside = beside + gathered(1, 0, 0)
        if i == half_r - 1:
            beside = beside + gathered(1, 1, 0)
        correction.append(
            (2.0 - relaxation) * guess[i] + c_inv[i] * (0.25 * beside + column)
        )

    stage_coarse(2, correction)
    start(2)
    c_up = [upper(x) for x in correction]
    c_down = [lower(x) for x in correction]

    def base(y, b):
        i = y // 2
        total = off[y][b] + 2.0 * correction[i]
        total = total + vertical[y][b] * c_up[i] + low_vert[y][b] * c_down[i]
        other = i - 1 if y % 2 == 0 else i + 1
        if 0 <= other < half_r:
            total = total + correction[other]
        return (
            (2.0 - relaxation) * smoothed[y][b] + (1.0 - relaxation) * correction[i],
            total,
        )

    bases = fine(base)
    for i in small:
        for p in range(panels):
            corr_ref[p, i] = correction[i][:half_c, p * levels : (p + 1) * levels]
    receive(2, half_r)
    left = [from_left(correction[i], nb_col[2, 0, i : i + 1, :]) for i in small]
    right = [from_right(correction[i], nb_col[2, 1, i : i + 1, :]) for i in small]
    top = gathered(2, 0, 0)
    bottom = gathered(2, 1, 0)
    for y, b in every:
        first, total = bases[y][b]
        total = total + (left if b == 0 else right)[y // 2]
        if y == 0:
            total = total + top
        if y == rows - 1:
            total = total + bottom
        spread[y, pl.ds(b, height, stride=2), :] = first + inverse[y][b] * total
    for p in range(panels):
        sol_ref[p] = spread[:, :cols, p * levels : (p + 1) * levels]
    for n in range(3):
        finish_sends(n)


def solution(mesh):
    nr, nc = mesh.shape["tx"], mesh.shape["ty"]

    def shards(residual, density, gain, vertical, edge_panel, edge_side, edge_flip):
        panels, rows, cols, levels = residual.shape
        k = cols // rows
        assert cols == k * rows and rows % 2 == 0 and panels * levels <= LANES
        seg_h = round_up(rows, 8)
        height = round_up(cols // 2, 8)
        tall = 2 * height
        f32 = jnp.float32
        return pl.pallas_call(
            functools.partial(kernel, nr, nc),
            out_shape=(
                jax.ShapeDtypeStruct(residual.shape, f32),
                jax.ShapeDtypeStruct((panels, rows // 2, cols // 2, levels), f32),
            ),
            in_specs=[pl.BlockSpec(memory_space=pl.ANY)] * 4
            + [pl.BlockSpec(memory_space=pltpu.SMEM)] * 3,
            out_specs=(pl.BlockSpec(memory_space=pltpu.VMEM),) * 2,
            scratch_shapes=[
                pltpu.VMEM((4, panels, rows, cols, levels), f32),
                pltpu.VMEM((3, rows, tall, LANES), f32),
                pltpu.VMEM((rows, tall, LANES), f32),
                pltpu.VMEM((4, 2, k, seg_h, LANES), f32),
                pltpu.VMEM((4, 2, seg_h, LANES), f32),
                pltpu.VMEM((4, 2, k, seg_h, LANES), f32),
                pltpu.VMEM((4, 2, seg_h, LANES), f32),
                pltpu.VMEM((3, 8, k, seg_h, LANES), f32),
                pltpu.VMEM((3, 8, seg_h, LANES), f32),
                pltpu.SemaphoreType.DMA((4,)),
                pltpu.SemaphoreType.DMA((3, 4 + 8 * k + 4 + 4)),
                pltpu.SemaphoreType.DMA((3, 4)),
                pltpu.SemaphoreType.DMA((3, 8, k)),
                pltpu.SemaphoreType.DMA((3, 8)),
            ],
            compiler_params=pltpu.CompilerParams(collective_id=0, has_side_effects=True),
        )(residual, density, gain, vertical, edge_panel.T, edge_side.T, edge_flip.T)

    fields = P(None, "tx", "ty", None)
    return jax.shard_map(
        shards,
        mesh=mesh,
        in_specs=(fields,) * 4 + (P(),) * 3,
        out_specs=(fields, fields),
        check_vma=False,
    )
```

```python
import functools

import jax
import jax.numpy as jnp
from jax import lax
from jax.experimental import pallas as pl
from jax.experimental.pallas import tpu as pltpu
from jax.sharding import PartitionSpec as P

MESH = pl.DeviceIdType.MESH
relaxation = 0.8
LANES = 128


def round_up(value, unit):
    return (value + unit - 1) // unit * unit


def kernel(
    nr,
    nc,
    res_hbm,
    den_hbm,
    gain_hbm,
    vert_hbm,
    panel_ref,
    side_ref,
    flip_ref,
    spread,
    small_ref,
    inp,
    packed,
    st_row,
    st_col,
    nb_row,
    nb_col,
    rx_row,
    rx_col,
    in_sem,
    send_sem,
    nb_sem,
    row_sem,
    col_sem,
):
    _, panels, rows, cols, levels = inp.shape
    half_r, half_c = rows // 2, cols // 2
    k = cols // rows
    height = spread.shape[1] // 2
    r = lax.axis_index("tx")
    c = lax.axis_index("ty")
    is_row = (r == 0) | (r == nr - 1)
    is_col = (c == 0) | (c == nc - 1)
    tr = r // (nr - 1)
    tc = c // (nc - 1)

    def messages(n):
        found = []
        for i in range(k):
            src = st_row.at[n, tr, i]
            for f in range(2):
                slot = 4 * f + tr
                i_dst = i if f == 0 else k - 1 - i
                c_dst = c if f == 0 else nc - 1 - c
                r_dst = k * c + i if f == 0 else nr - 1 - k * c - i
                for e in range(2):
                    found.append(
                        (
                            is_row,
                            (e * (nr - 1), c_dst),
                            src,
                            rx_row.at[n, slot, i_dst],
                            row_sem.at[n, slot, i_dst],
                        )
                    )
                    found.append(
                        (
                            is_row,
                            (r_dst, e * (nc - 1)),
                            src,
                            rx_col.at[n, slot],
                            col_sem.at[n, slot],
                        )
                    )
        src = st_col.at[n, tc]
        for f in range(2):
            slot = 4 * f + 2 + tc
            g = r if f == 0 else nr - 1 - r
            for e in range(2):
                found.append(
                    (
                        is_col,
                        (e * (nr - 1), g // k),
                        src,
                        rx_row.at[n, slot, g % k],
                        row_sem.at[n, slot, g % k],
                    )
                )
                found.append(
                    (is_col, (g, e * (nc - 1)), src, rx_col.at[n, slot], col_sem.at[n, slot])
                )
        found.append((r > 0, (r - 1, c), st_row.at[n, 0], nb_row.at[n, 1], nb_sem.at[n, 1]))
        found.append((r < nr - 1, (r + 1, c), st_row.at[n, 1], nb_row.at[n, 0], nb_sem.at[n, 0]))
        found.append((c > 0, (r, c - 1), st_col.at[n, 0], nb_col.at[n, 1], nb_sem.at[n, 3]))
        found.append((c < nc - 1, (r, c + 1), st_col.at[n, 1], nb_col.at[n, 0], nb_sem.at[n, 2]))
        return found

    def same(dest):
        return (dest[0] == r) & (dest[1] == c)

    barrier = pltpu.get_barrier_semaphore()
    expected = jnp.int32(0)
    for active, dest, _, _, _ in messages(0):
        go = active & jnp.logical_not(same(dest))
        expected = expected + go.astype(jnp.int32)

        @pl.when(go)
        def _():
            pl.semaphore_signal(barrier, inc=1, device_id=dest, device_id_type=MESH)

    loads = [
        pltpu.make_async_copy(source, inp.at[i], in_sem.at[i])
        for i, source in enumerate((den_hbm, res_hbm, gain_hbm, vert_hbm))
    ]
    for load in loads:
        load.start()

    lane = lax.broadcasted_iota(jnp.int32, (height, LANES), 1)
    sub = lax.broadcasted_iota(jnp.int32, (height, LANES), 0)
    level = lane % levels
    first_level = level == 0
    last_level = level == levels - 1

    def lower(x):
        return jnp.where(first_level, 0.0, pltpu.roll(x, 1, 1))

    def upper(x):
        return jnp.where(last_level, 0.0, pltpu.roll(x, LANES - 1, 1))

    seg_h = st_col.shape[2]
    seg_lane = lax.broadcasted_iota(jnp.int32, (seg_h, LANES), 1)

    def pick_tables(side):
        index = seg_lane
        code = jnp.zeros_like(seg_lane)
        for p in range(panels):
            here = seg_lane // levels == p
            index = jnp.where(here, panel_ref[side, p] * levels + seg_lane % levels, index)
            code = jnp.where(here, flip_ref[side, p] * 4 + side_ref[side, p], code)
        return index, code

    row_pick = pick_tables(tr)
    col_pick = pick_tables(2 + tc)

    for load in loads:
        load.wait()

    def pack(value):
        filler = jnp.zeros((rows, cols, LANES - panels * levels), jnp.float32)
        return jnp.concatenate([value[p] for p in range(panels)] + [filler], axis=-1)

    def split(which, value):
        packed[which, :, :cols, :] = value
        if packed.shape[2] > cols:
            packed[which, :, cols:, :] = jnp.zeros(
                (rows, packed.shape[2] - cols, LANES), jnp.float32
            )
        return [
            [packed[which, y, pl.ds(b, height, stride=2), :] for b in range(2)]
            for y in range(rows)
        ]

    every = [(y, b) for y in range(rows) for b in range(2)]

    def fine(fun):
        return [[fun(y, b) for b in range(2)] for y in range(rows)]

    right_side = split(0, pack(inp[0] * inp[1]))
    gain = split(1, pack(inp[2]))
    vertical = split(2, pack(inp[3]))
    low_vert = fine(lambda y, b: lower(vertical[y][b]))
    inverse = fine(
        lambda y, b: relaxation / (gain[y][b] + 4.0 + vertical[y][b] + low_vert[y][b])
    )
    smoothed = fine(lambda y, b: inverse[y][b] * right_side[y][b])

    def start(n):
        for m, (active, dest, src, dst, sem) in enumerate(messages(n)):
            mine = same(dest)

            @pl.when(active & jnp.logical_not(mine))
            def _():
                pltpu.make_async_remote_copy(
                    src_ref=src,
                    dst_ref=dst,
                    send_sem=send_sem.at[n, m],
                    recv_sem=sem,
                    device_id=dest,
                    device_id_type=MESH,
                ).start()

            if m < 8 * k + 8:

                @pl.when(active & mine)
                def _():
                    pltpu.make_async_copy(src, dst, sem).start()

    def finish_sends(n):
        for m, (active, dest, src, dst, sem) in enumerate(messages(n)):

            @pl.when(active & jnp.logical_not(same(dest)))
            def _():
                pltpu.make_async_copy(src, src, send_sem.at[n, m]).wait()

    def mirrored(x, length):
        lines = [x[length - 1 - s : length - s] for s in range(length)]
        if seg_h > length:
            lines.append(jnp.zeros((seg_h - length, LANES), jnp.float32))
        return jnp.concatenate(lines, axis=0)

    def select(read, pick, length):
        index, code = pick
        parts = []
        for f in range(2):
            taken = jnp.zeros((seg_h, LANES), jnp.float32)
            for t in range(4):
                moved = jnp.take_along_axis(
                    read(4 * f + t), index, axis=1, mode="promise_in_bounds"
                )
                taken = jnp.where(code == 4 * f + t, moved, taken)
            parts.append(taken)
        return jnp.where(code >= 4, mirrored(parts[1], length), parts[0])

    def receive(n, length):
        def arrived(ref, sem):
            pltpu.make_async_copy(ref, ref, sem).wait()

        @pl.when(r > 0)
        def _():
            arrived(nb_row.at[n, 0], nb_sem.at[n, 0])

        @pl.when(r < nr - 1)
        def _():
            arrived(nb_row.at[n, 1], nb_sem.at[n, 1])

        @pl.when(c > 0)
        def _():
            arrived(nb_col.at[n, 0], nb_sem.at[n, 2])

        @pl.when(c < nc - 1)
        def _():
            arrived(nb_col.at[n, 1], nb_sem.at[n, 3])

        @pl.when(is_row)
        def _():
            for slot in range(8):
                for i in range(k):
                    arrived(rx_row.at[n, slot, i], row_sem.at[n, slot, i])
            for i in range(k):
                nb_row[n, tr, i] = select(lambda s: rx_row[n, s, i], row_pick, length)

        @pl.when(is_col)
        def _():
            for slot in range(8):
                arrived(rx_col.at[n, slot], col_sem.at[n, slot])
            nb_col[n, tc] = select(lambda s: rx_col[n, s], col_pick, length)

    def gathered(n, end, b):
        lines = [nb_row[n, end, i, b * half_r : (b + 1) * half_r, :] for i in range(k)]
        if height > half_c:
            lines.append(jnp.zeros((height - half_c, LANES), jnp.float32))
        return jnp.concatenate(lines, axis=0)

    def from_left(x, line):
        return jnp.where(sub == 0, line, pltpu.roll(x, 1, 0))

    def from_right(x, line):
        return jnp.where(sub == half_c - 1, line, pltpu.roll(x, height - 1, 0))

    for end, y in ((0, 0), (1, rows - 1)):
        for i in range(k):
            for b in range(2):
                st_row[0, end, i, b * half_r : (b + 1) * half_r, :] = smoothed[y][b][
                    i * half_r : (i + 1) * half_r
                ]
    for y in range(rows):
        at = (y % 2) * half_r + y // 2
        st_col[0, 0, at : at + 1, :] = smoothed[y][0][0:1]
        st_col[0, 1, at : at + 1, :] = smoothed[y][1][half_c - 1 : half_c]
    pl.semaphore_wait(barrier, expected)
    start(0)

    def inner(y, b):
        x = smoothed[y][b]
        total = vertical[y][b] * upper(x) + low_vert[y][b] * lower(x) + smoothed[y][1 - b]
        if y > 0:
            total = total + smoothed[y - 1][b]
        if y < rows - 1:
            total = total + smoothed[y + 1][b]
        return total

    partial = fine(inner)

    def block_mean(values, i):
        y = 2 * i
        return 0.25 * (values[y][0] + values[y][1] + values[y + 1][0] + values[y + 1][1])

    small = range(half_r)
    c_vert = [block_mean(vertical, i) for i in small]
    c_low = [lower(c_vert[i]) for i in small]
    c_inv = [relaxation / (block_mean(gain, i) + 1.0 + c_vert[i] + c_low[i]) for i in small]

    receive(0, rows)

    def outer(y, b):
        at = (y % 2) * half_r + y // 2
        if b == 0:
            total = partial[y][b] + from_left(smoothed[y][1], nb_col[0, 0, at : at + 1, :])
        else:
            total = partial[y][b] + from_right(smoothed[y][0], nb_col[0, 1, at : at + 1, :])
        if y == 0:
            total = total + gathered(0, 0, b)
        if y == rows - 1:
            total = total + gathered(0, 1, b)
        return total

    off = fine(outer)
    residual = fine(lambda y, b: (1.0 - relaxation) * right_side[y][b] + off[y][b])
    guess = [c_inv[i] * block_mean(residual, i) for i in small]

    def stage_coarse(n, values):
        for end, i in ((0, 0), (1, half_r - 1)):
            for piece in range(k):
                st_row[n, end, piece, :half_r, :] = values[i][
                    piece * half_r : (piece + 1) * half_r
                ]
        for i in small:
            st_col[n, 0, i : i + 1, :] = values[i][0:1]
            st_col[n, 1, i : i + 1, :] = values[i][half_c - 1 : half_c]

    stage_coarse(1, guess)
    start(1)
    c_partial = []
    for i in small:
        x = guess[i]
        beside = jnp.zeros_like(x)
        if i > 0:
            beside = beside + guess[i - 1]
        if i < half_r - 1:
            beside = beside + guess[i + 1]
        c_partial.append(
            (beside, c_vert[i] * upper(x) + c_low[i] * lower(x))
        )
    receive(1, half_r)
    correction = []
    for i in small:
        beside, column = c_partial[i]
        beside = beside + from_left(guess[i], nb_col[1, 0, i : i + 1, :])
        beside = beside + from_right(guess[i], nb_col[1, 1, i : i + 1, :])
        if i == 0:
            beside = beside + gathered(1, 0, 0)
        if i == half_r - 1:
            beside = beside + gathered(1, 1, 0)
        correction.append(
            (2.0 - relaxation) * guess[i] + c_inv[i] * (0.25 * beside + column)
        )

    stage_coarse(2, correction)
    start(2)
    c_up = [upper(x) for x in correction]
    c_down = [lower(x) for x in correction]

    def base(y, b):
        i = y // 2
        total = off[y][b] + 2.0 * correction[i]
        total = total + vertical[y][b] * c_up[i] + low_vert[y][b] * c_down[i]
        other = i - 1 if y % 2 == 0 else i + 1
        if 0 <= other < half_r:
            total = total + correction[other]
        return (
            (2.0 - relaxation) * smoothed[y][b] + (1.0 - relaxation) * correction[i],
            total,
        )

    bases = fine(base)
    for i in small:
        small_ref[i] = correction[i]
    receive(2, half_r)
    left = [from_left(correction[i], nb_col[2, 0, i : i + 1, :]) for i in small]
    right = [from_right(correction[i], nb_col[2, 1, i : i + 1, :]) for i in small]
    top = gathered(2, 0, 0)
    bottom = gathered(2, 1, 0)
    for y, b in every:
        first, total = bases[y][b]
        total = total + (left if b == 0 else right)[y // 2]
        if y == 0:
            total = total + top
        if y == rows - 1:
            total = total + bottom
        spread[y, pl.ds(b, height, stride=2), :] = first + inverse[y][b] * total
    for n in range(3):
        finish_sends(n)


def unpack(spread, small_ref, sol_ref, corr_ref):
    panels, _, cols, levels = sol_ref.shape
    half_c = corr_ref.shape[2]
    for p in range(panels):
        lanes = slice(p * levels, (p + 1) * levels)
        sol_ref[p] = spread[:, :cols, lanes]
        corr_ref[p] = small_ref[:, :half_c, lanes]


def solution(mesh):
    nr, nc = mesh.shape["tx"], mesh.shape["ty"]

    def shards(residual, density, gain, vertical, edge_panel, edge_side, edge_flip):
        panels, rows, cols, levels = residual.shape
        k = cols // rows
        assert cols == k * rows and rows % 2 == 0 and panels * levels <= LANES
        seg_h = round_up(rows, 8)
        height = round_up(cols // 2, 8)
        tall = 2 * height
        f32 = jnp.float32
        spread, small = pl.pallas_call(
            functools.partial(kernel, nr, nc),
            out_shape=(
                jax.ShapeDtypeStruct((rows, tall, LANES), f32),
                jax.ShapeDtypeStruct((rows // 2, height, LANES), f32),
            ),
            in_specs=[pl.BlockSpec(memory_space=pl.ANY)] * 4
            + [pl.BlockSpec(memory_space=pltpu.SMEM)] * 3,
            out_specs=(pl.BlockSpec(memory_space=pltpu.VMEM),) * 2,
            scratch_shapes=[
                pltpu.VMEM((4, panels, rows, cols, levels), f32),
                pltpu.VMEM((3, rows, tall, LANES), f32),
                pltpu.VMEM((4, 2, k, seg_h, LANES), f32),
                pltpu.VMEM((4, 2, seg_h, LANES), f32),
                pltpu.VMEM((4, 2, k, seg_h, LANES), f32),
                pltpu.VMEM((4, 2, seg_h, LANES), f32),
                pltpu.VMEM((3, 8, k, seg_h, LANES), f32),
                pltpu.VMEM((3, 8, seg_h, LANES), f32),
                pltpu.SemaphoreType.DMA((4,)),
                pltpu.SemaphoreType.DMA((3, 4 + 8 * k + 4 + 4)),
                pltpu.SemaphoreType.DMA((3, 4)),
                pltpu.SemaphoreType.DMA((3, 8, k)),
                pltpu.SemaphoreType.DMA((3, 8)),
            ],
            compiler_params=pltpu.CompilerParams(collective_id=0, has_side_effects=True),
        )(residual, density, gain, vertical, edge_panel.T, edge_side.T, edge_flip.T)
        return pl.pallas_call(
            unpack,
            out_shape=(
                jax.ShapeDtypeStruct(residual.shape, f32),
                jax.ShapeDtypeStruct((panels, rows // 2, cols // 2, levels), f32),
            ),
            in_specs=[pl.BlockSpec(memory_space=pltpu.VMEM)] * 2,
            out_specs=(pl.BlockSpec(memory_space=pltpu.VMEM),) * 2,
        )(spread, small)

    fields = P(None, "tx", "ty", None)
    return jax.shard_map(
        shards,
        mesh=mesh,
        in_specs=(fields,) * 4 + (P(),) * 3,
        out_specs=(fields, fields),
        check_vma=False,
    )
```
